256 devices in a mesh: tm: 32 (over y, z), row: 8 (over x, core).
Axes of the slice: x: 4, y: 4, z: 8, core: 2. Of those that a mesh axis runs over, the one named last changes fastest.
Arguments:
- precisions: float32 [32, 1024, 1024], P('tm', 'row'), as said below
- couplings: float32 [32, 1024, 1024], P('tm', 'row'), as said below
- right_sides: float32 [32, 1024, 256], P('tm', 'row'), may hold values from -6 to 6
Outputs:
- pivot_blocks: float32 [32, 1024, 1024], P('tm', 'row')
- coupling_blocks: float32 [32, 1024, 1024], P('tm', 'row')
- reduced_sides: float32 [32, 1024, 256], P('tm', 'row')
The draws below stay inside these ranges and needn't reach their ends.
Inputs may be any that keep to these rules, and one draw needn't show every extreme that they name: precisions and couplings together form a symmetric positive definite block-tridiagonal matrix whose eigenvalues are 1 or more; couplings[0] is zero. `couplings`: see precisions.
All inputs are finite; a program needn't handle non-finite values.
Results may differ from the reference program's by a relative error of at most 0.00023.
Values sent between devices are 32-bit elements; how exact they have to be, the bound alone decides.
No kernel may reach another device: no remote copies, remote signals or barrier semaphores. Data moves between devices by JAX's collectives and lax.ppermute only.
A program may use at most 128 MiB of HBM per device.

```python
import math
import jax
import jax.numpy as jnp
from jax import lax

D = 1024
RHS_COLS = 256
LEVELS = 2
BLOCKS = 32


def lag_factors(base_key):
    seeded = jax.random.fold_in(base_key, 11)
    gain_key, diag_key, lag_key = jax.random.split(seeded, 3)
    scale = 0.5 / math.sqrt(D)
    gains = jax.random.uniform(gain_key, (BLOCKS, D), jnp.float32, 1.0, 2.0)
    diag_noise = jax.random.normal(diag_key, (BLOCKS, D, D), jnp.float32)
    lag_noise = jax.random.normal(lag_key, (BLOCKS, D, D), jnp.float32)
    identity = jnp.eye(D, dtype=jnp.float32)
    diag_factor = gains[:, :, None] * identity[None, :, :] + scale * diag_noise
    later = (jnp.arange(BLOCKS) > 0).astype(jnp.float32)
    lag_factor = (0.9 * identity[None, :, :] + scale * lag_noise) * later[:, None, None]
    return (diag_factor, lag_factor)


def draw_precisions(key, part):
    diag_factor, lag_factor = lag_factors(key)
    exact = lax.Precision.HIGHEST
    own = jnp.einsum('tij,tkj->tik', diag_factor, diag_factor, precision=exact)
    lagged = jnp.einsum('tij,tkj->tik', lag_factor, lag_factor, precision=exact)
    identity = jnp.eye(D, dtype=jnp.float32)
    return own + lagged + identity[None, :, :]


def draw_couplings(key, part):
    diag_factor, lag_factor = lag_factors(key)
    earlier = jnp.roll(diag_factor, 1, axis=0)
    return jnp.einsum('tij,tkj->tik', earlier, lag_factor, precision=lax.Precision.HIGHEST)


def block_scale(key, dims, pieces, low, high):
    def one(position, shards_of):
        draws = jax.random.uniform(jax.random.fold_in(jax.random.fold_in(key, 6), position), (shards_of,), jnp.float32, low / len(pieces), high / len(pieces))
        return jnp.repeat(jnp.exp(draws), dims[position] // shards_of).reshape((-1,) + (1,) * (len(dims) - position - 1))

    factor_of = one(*pieces[0])
    for cut in pieces[1:]:
        factor_of = factor_of * one(*cut)
    return factor_of


def centred(stream_key, extent, deviation, reach, shards=(), kind=jnp.bfloat16):
    array = deviation * jax.random.normal(stream_key, extent, jnp.float32)
    if shards:
        array = array * block_scale(stream_key, extent, shards, -0.22, 0.18)
    return jnp.clip(array, -reach, reach).astype(kind)


def setup_inputs(seed: int = 0) -> dict:
    seeds = jax.random.split(jax.random.key(seed), 4)
    return {
        "precisions": draw_precisions(jax.random.fold_in(seeds[3], 71), 0),
        "couplings": draw_couplings(jax.random.fold_in(seeds[3], 71), 0),
        "right_sides": centred(seeds[2], (BLOCKS, D, RHS_COLS), 1.0, 6.0, ((0, 32), (1, 8)), jnp.float32),
    }


def product(left, right):
    return lax.dot_general(left, right, (((0,), (0,)), ((), ())), precision=lax.Precision.HIGHEST)

def reference(precisions, couplings, right_sides):
    block_count = precisions.shape[0]
    pivot_list = [precisions[block_index] for block_index in range(block_count)]
    coupling_list = [jnp.zeros_like(couplings[0])] + [couplings[block_index] for block_index in range(1, block_count)]
    side_list = [right_sides[block_index] for block_index in range(block_count)]
    for level_step in range(LEVELS):
        level_stride = 2 ** level_step
        new_pivots = list(pivot_list)
        new_couplings = list(coupling_list)
        new_sides = list(side_list)
        for middle in range(block_count):
            lower_fac = jnp.linalg.cholesky(pivot_list[middle])
            left_solve = jax.scipy.linalg.solve_triangular(lower_fac, coupling_list[middle].T, lower=True)
            side_solve = jax.scipy.linalg.solve_triangular(lower_fac, side_list[middle], lower=True)
            before = middle - level_stride
            if before >= 0:
                new_pivots[before] = new_pivots[before] - product(left_solve, left_solve)
                new_sides[before] = new_sides[before] - product(left_solve, side_solve)
            after_index = middle + level_stride
            if after_index < block_count:
                right_solve = jax.scipy.linalg.solve_triangular(lower_fac, coupling_list[after_index], lower=True)
                new_pivots[after_index] = new_pivots[after_index] - product(right_solve, right_solve)
                new_sides[after_index] = new_sides[after_index] - product(right_solve, side_solve)
                new_couplings[after_index] = -product(left_solve, right_solve)
        for early in range(min(level_stride, block_count)):
            new_couplings[early] = jnp.zeros_like(coupling_list[early])
        pivot_list = new_pivots
        coupling_list = new_couplings
        side_list = new_sides
    return (jnp.stack(pivot_list), jnp.stack(coupling_list), jnp.stack(side_list))
```

```python
import functools
import jax
import jax.numpy as jnp
from jax import lax
from jax.experimental import pallas as pl
from jax.experimental.pallas import tpu as pltpu
from jax.sharding import PartitionSpec as P

LEVELS = 2
BLK = 256
F32, BF16 = jnp.float32, jnp.bfloat16
OFFSETS = ((0, 0), (-1, 0), (1, 0), (2, 0), (0, 1), (-1, 1), (1, 1), (2, 1))
NN, NT, TN = (((1,), (0,)), ((), ())), (((1,), (1,)), ((), ())), (((0,), (0,)), ((), ()))


def split(x):
    high = x.astype(BF16)
    return high, (x - high.astype(F32)).astype(BF16)


def dot(a, b, dims):
    return lax.dot_general(a, b, dims, preferred_element_type=F32)


def dot3(a, b, dims=NN):
    (ah, al), (bh, bl) = a, b
    return dot(ah, bh, dims) + (dot(ah, bl, dims) + dot(al, bh, dims))


def exact(a, b):
    return lax.dot_general(a, b, NN, precision=lax.Precision.HIGHEST, preferred_element_type=F32)


def places(row):
    chip, core = row // 2, row % 2
    return [((chip + dx + 4) % 4) * 2 + (core if dc == 0 else 1 - core) for dx, dc in OFFSETS]


def eye(n):
    return (lax.broadcasted_iota(jnp.int32, (n, n), 0) == lax.broadcasted_iota(jnp.int32, (n, n), 1)).astype(F32)


def invert_small(block, x_ref, e_ref):
    n = block.shape[0]
    one = eye(n)
    top = jnp.max(jnp.sum(jnp.abs(block), axis=0))
    scale = 2.0 / (1.0 + top)
    bound = (top - 1.0) / (top + 1.0)
    e_ref[...] = one - scale * block
    x_ref[...] = scale * one

    def coupled(carry):
        count, bound = carry
        square = bound * bound
        gain = 2.0 / (2.0 - square)
        x, e = x_ref[...], e_ref[...]
        es = split(e)
        x_ref[...] = gain * (x + dot3(split(x), es))
        e_ref[...] = gain * dot3(es, es) + (1.0 - gain) * one
        return count + 1, square / (2.0 - square)

    lax.while_loop(lambda c: (c[0] < 40) & (c[1] > 1e-3), coupled, (0, bound))

    def residual(carry):
        count, _ = carry
        x = x_ref[...]
        e = one - exact(x, block)
        x_ref[...] = x + dot3(split(x), split(e))
        return count + 1, jnp.max(jnp.sum(jnp.abs(e), axis=0))

    lax.while_loop(lambda c: (c[0] < 20) & (c[1] > 5e-3), residual, (0, jnp.float32(1.0)))


def inverse_kernel(own, r, l, f, xown, xrl, xf, high_ref, low_ref, a_ref, x_ref, e_ref, ch_ref, cl_ref, wh_ref, wl_ref):
    n = a_ref.shape[0]
    rows = own.shape[0]
    where = places(lax.axis_index("row"))
    parts = (own[:, :n], r[:, :n], l[:, :n], f[:, :n], xown[:, :n], xrl[:rows, :n], xrl[rows:, :n], xf[:, :n])
    for place, part in zip(where, parts):
        a_ref[pl.ds(pl.multiple_of(place * rows, rows), rows), :] = part
    blocks = n // BLK

    @pl.loop(0, blocks)
    def _(k):
        ks = pl.ds(pl.multiple_of(k * BLK, BLK), BLK)
        invert_small(a_ref[ks, ks], x_ref, e_ref)
        a_ref[ks, ks] = -eye(BLK)
        xs = split(x_ref[...])
        ws = split(dot3(xs, split(a_ref[ks, :])))
        wh_ref[...], wl_ref[...] = ws
        ch, cl = split(a_ref[:, ks])
        ch_ref[...] = ch
        cl_ref[...] = cl

        @pl.loop(1, blocks)
        def _(step):
            i = lax.rem(k + step, blocks)
            rs = pl.ds(pl.multiple_of(i * BLK, BLK), BLK)
            a_ref[rs, ks] = jnp.zeros((BLK, BLK), F32)
            c = ch_ref[rs, :], cl_ref[rs, :]
            for j in range(blocks):
                js = slice(j * BLK, (j + 1) * BLK)
                a_ref[rs, js] = a_ref[rs, js] - dot3(c, (wh_ref[:, js], wl_ref[:, js]))

        a_ref[ks, :] = wh_ref[...].astype(F32) + wl_ref[...].astype(F32)

    @pl.loop(0, blocks)
    def _(i):
        rs = pl.ds(pl.multiple_of(i * BLK, BLK), BLK)
        high_ref[rs, :], low_ref[rs, :] = split(-a_ref[rs, :])


VMEM = pl.BlockSpec(memory_space=pltpu.VMEM)
LIMIT = 56 << 20


def inverse(chunks, n):
    half = jax.ShapeDtypeStruct((n, n), BF16)
    return pl.pallas_call(
        inverse_kernel,
        out_shape=(half, half),
        in_specs=[VMEM] * 7,
        out_specs=(VMEM, VMEM),
        scratch_shapes=[
            pltpu.VMEM((n, n), F32),
            pltpu.VMEM((BLK, BLK), F32),
            pltpu.VMEM((BLK, BLK), F32),
            pltpu.VMEM((n, BLK), BF16),
            pltpu.VMEM((n, BLK), BF16),
            pltpu.VMEM((BLK, n), BF16),
            pltpu.VMEM((BLK, n), BF16),
        ],
        compiler_params=pltpu.CompilerParams(vmem_limit_bytes=LIMIT),
        cost_estimate=pl.CostEstimate(flops=20 * n**3, bytes_accessed=8 * n * n, transcendentals=0),
        name="inverse",
    )(*chunks)


def pieces(refs, rows, lo, hi):
    own, r, l, f, xown, xrl, xf = refs
    return [
        own.at[:, lo:hi], r.at[:, lo:hi], l.at[:, lo:hi], f.at[:, lo:hi], xown.at[:, lo:hi],
        xrl.at[pl.ds(0, rows), lo:hi], xrl.at[pl.ds(rows, rows), lo:hi], xf.at[:, lo:hi],
    ]


def earlier_kernel(xh, xl, *refs):
    chunks, (out, g_ref) = refs[:7], refs[7:]
    rows, n = out.shape[0], xh.shape[0]
    where = places(lax.axis_index("row"))
    own = split(chunks[0][:, :n])
    g_ref[...] = dot3(own, (xh[...], xl[...]))
    g = split(g_ref[...])
    side = jnp.zeros((rows, out.shape[1] - n), F32)
    for place, link, rhs in zip(where, pieces(chunks, rows, 0, n), pieces(chunks, rows, n, out.shape[1])):
        cols = pl.ds(pl.multiple_of(place * rows, rows), rows)
        out[:, cols] = dot3(g, split(link[...]), NT)
        side += dot3(split(g_ref[:, cols]), split(rhs[...]))
    out[:, n:] = side


def later_kernel(xh, xl, prior, *refs):
    links, sides = refs[:7], refs[7:14]
    coupling, term, whole_h, whole_l, h_ref = refs[14:]
    rows, n = coupling.shape[0], xh.shape[0]
    where = places(lax.axis_index("row"))
    me = pl.ds(pl.multiple_of(lax.axis_index("row") * rows, rows), rows)
    for place, link in zip(where, pieces(links, rows, 0, n)):
        at = pl.ds(pl.multiple_of(place * rows, rows), rows)
        whole_h[at, :], whole_l[at, :] = split(link[...])
    x = xh[...], xl[...]
    h_ref[:rows] = dot3(split(prior[:, :n]), x)
    h_ref[rows:] = dot3((whole_h[:, me], whole_l[:, me]), x, TN)
    h = split(h_ref[...])
    for j in range(n // BLK):
        js = slice(j * BLK, (j + 1) * BLK)
        both = dot3(h, (whole_h[:, js], whole_l[:, js]))
        coupling[:, js] = -both[:rows]
        term[:, js] = both[rows:]
    side = jnp.zeros((rows, term.shape[1] - n), F32)
    for place, rhs in zip(where, pieces(sides, rows, n, term.shape[1])):
        cols = pl.ds(pl.multiple_of(place * rows, rows), rows)
        side += dot3(split(h_ref[rows:, cols]), split(rhs[...]))
    term[:, n:] = side


def earlier(x, chunks):
    rows, width = chunks[0].shape
    n = x[0].shape[0]
    return pl.pallas_call(
        earlier_kernel,
        out_shape=jax.ShapeDtypeStruct((rows, width), F32),
        in_specs=[VMEM] * 9,
        out_specs=VMEM,
        scratch_shapes=[pltpu.VMEM((rows, n), F32)],
        compiler_params=pltpu.CompilerParams(vmem_limit_bytes=LIMIT),
        cost_estimate=pl.CostEstimate(flops=6 * rows * n * (n + width), bytes_accessed=8 * n * n, transcendentals=0),
        name="earlier",
    )(*x, *chunks)


def later(x, prior, links, sides):
    rows, width = links[0].shape
    n = x[0].shape[0]
    return pl.pallas_call(
        later_kernel,
        out_shape=(jax.ShapeDtypeStruct((rows, n), F32), jax.ShapeDtypeStruct((rows, width), F32)),
        in_specs=[VMEM] * 17,
        out_specs=(VMEM, VMEM),
        scratch_shapes=[pltpu.VMEM((n, n), BF16), pltpu.VMEM((n, n), BF16), pltpu.VMEM((2 * rows, n), F32)],
        compiler_params=pltpu.CompilerParams(vmem_limit_bytes=LIMIT),
        cost_estimate=pl.CostEstimate(flops=12 * rows * n * (n + width), bytes_accessed=8 * n * n, transcendentals=0),
        name="later",
    )(*x, prior, *links, *sides)


def after(value, *others):
    return lax.optimization_barrier((value, *others))[0]


def gather(rows, extra=()):
    core = lax.axis_index("row") % 2
    devices = range(8)

    def send(value, to):
        return lax.ppermute(value, "row", [(i, to(i)) for i in devices])

    r = send(rows, lambda i: (i + 2) % 8)
    l = send(rows, lambda i: (i - 2) % 8)
    xown = send(rows, lambda i: i ^ 1)
    f = send(jnp.where(core == 0, r, l), lambda i: (i + 2) % 8 if i % 2 == 0 else (i - 2) % 8)
    xrl = send(jnp.concatenate([r, l]), lambda i: i ^ 1)
    xf = send(f, lambda i: i ^ 1)
    return rows, r, l, f, xown, xrl, xf


def local(precisions, couplings, right_sides):
    pivot, link, side = precisions[0], couplings[0], right_sides[0]
    n = pivot.shape[1]
    count = lax.axis_size("tm")
    link = jnp.where(lax.axis_index("tm") == 0, jnp.zeros_like(link), link)
    for level in range(LEVELS):
        h = 1 << level
        ring = [(i, (i + h) % count) for i in range(count)]
        line = [(i, i - h) for i in range(h, count)]
        before_p = lax.ppermute(pivot, "tm", ring)
        linkside = jnp.concatenate([link, side], axis=1)
        own_p = gather(pivot)
        before_l = lax.ppermute(after(linkside, before_p), "tm", ring)
        own_l = gather(after(linkside, own_p[3]))
        x = inverse(own_p, n)
        sent = earlier(x, own_l)
        got = lax.ppermute(sent, "tm", line)
        before = jnp.concatenate([before_p, before_l[:, n:]], axis=1)
        prior = gather(after(before, own_l[3]))
        x = inverse(prior, n)
        link, term = later(x, before_l, own_l, prior)
        pivot = pivot - got[:, :n] - term[:, :n]
        side = side - got[:, n:] - term[:, n:]
    return pivot[None], link[None], side[None]


def solution(mesh):
    placed = (P("tm", "row", None),) * 3
    return jax.shard_map(local, mesh=mesh, in_specs=placed, out_specs=placed, check_vma=False)
```

```python
import functools
import jax
import jax.numpy as jnp
from jax import lax
from jax.experimental import pallas as pl
from jax.experimental.pallas import tpu as pltpu
from jax.sharding import PartitionSpec as P

LEVELS = 2
BLK = 256
HALF = 5
COST = 1 << 33
F32, BF16 = jnp.float32, jnp.bfloat16
OFFSETS = ((0, 0), (-1, 0), (1, 0), (2, 0), (0, 1), (-1, 1), (1, 1), (2, 1))
NN, NT, TN = (((1,), (0,)), ((), ())), (((1,), (1,)), ((), ())), (((0,), (0,)), ((), ()))


def split(x):
    high = x.astype(BF16)
    return high, (x - high.astype(F32)).astype(BF16)


def dot(a, b, dims):
    return lax.dot_general(a, b, dims, preferred_element_type=F32)


def dot3(a, b, dims=NN):
    (ah, al), (bh, bl) = a, b
    return dot(ah, bh, dims) + (dot(ah, bl, dims) + dot(al, bh, dims))


def places(row):
    chip, core = row // 2, row % 2
    return [((chip + dx + 4) % 4) * 2 + (core if dc == 0 else 1 - core) for dx, dc in OFFSETS]


def eye(n):
    return (lax.broadcasted_iota(jnp.int32, (n, n), 0) == lax.broadcasted_iota(jnp.int32, (n, n), 1)).astype(F32)


def invert_small(block, x_ref, e_ref):
    one = eye(block.shape[0])
    top = jnp.max(jnp.sum(jnp.abs(block), axis=0))
    scale = 2.0 / (1.0 + top)
    bound = (top - 1.0) / (top + 1.0)
    square = bound * bound
    gain = 2.0 / (2.0 - square)
    e = one - scale * block
    es = split(e)
    x_ref[...] = (gain * scale) * (one + e)
    e_ref[...] = gain * dot3(es, es) + (1.0 - gain) * one

    def coupled(carry):
        count, bound = carry
        square = bound * bound
        gain = 2.0 / (2.0 - square)
        x, e = x_ref[...], e_ref[...]
        es = split(e)
        x_ref[...] = gain * (x + dot3(split(x), es))
        e_ref[...] = gain * dot3(es, es) + (1.0 - gain) * one
        return count + 1, square / (2.0 - square)

    lax.while_loop(lambda c: (c[0] < 40) & (c[1] > 1e-3), coupled, (0, square / (2.0 - square)))

    def residual(carry):
        count, _ = carry
        x = x_ref[...]
        xs = split(x)
        e = one - dot3(xs, split(block))
        x_ref[...] = x + dot3(xs, split(e))
        return count + 1, jnp.max(jnp.sum(jnp.abs(e), axis=0))

    lax.while_loop(lambda c: (c[0] < 20) & (c[1] > 1e-2), residual, (0, jnp.float32(1.0)))


def span(k, size=BLK):
    return pl.ds(pl.multiple_of(k * size, size), size)


def factor_kernel(lo, *refs):
    chunks, (high, low, a_ref, x_ref, e_ref, rows_ref) = refs[:8], refs[8:]
    n, rows, count = a_ref.shape[0], chunks[0].shape[0], rows_ref.shape[0]
    spread(chunks, lo, lo + HALF * rows, lambda place: rows_ref.at[place], rows)
    for k in range(count):
        for m in range(HALF):
            c = (k + m) % count
            block = rows_ref.at[k, :, m * rows:(m + 1) * rows]
            ki, ci = slice(k * rows, (k + 1) * rows), slice(c * rows, (c + 1) * rows)
            if c >= k:
                a_ref[ki, ci] = block[...]
            if (c < k and 2 * m < count) or (c == k + 1 and k % 2 == 0):
                a_ref[ci, ki] = block[...].T
    blocks = n // BLK

    @pl.loop(0, blocks)
    def _(k):
        ks = span(k)
        invert_small(a_ref[ks, ks], x_ref, e_ref)
        xs = split(x_ref[...])
        high[ks, ks], low[ks, ks] = xs

        @pl.loop(k + 1, blocks)
        def _(j):
            js = span(j)
            high[ks, js], low[ks, js] = split(dot3(xs, split(a_ref[ks, js])))

        @pl.loop(k + 1, blocks)
        def _(i):
            side = split(a_ref[ks, span(i)])

            @pl.loop(i, blocks)
            def _(j):
                js = span(j)
                a_ref[span(i), js] = a_ref[span(i), js] - dot3(side, (high[ks, js], low[ks, js]), TN)


def solve(z_ref, high, low):
    blocks = z_ref.shape[1] // BLK
    at = [slice(k * BLK, (k + 1) * BLK) for k in range(blocks)]
    halves = []
    for k in range(blocks):
        z = z_ref[:, at[k]]
        for i in range(k):
            z = z - dot3(halves[i], (high[at[i], at[k]], low[at[i], at[k]]))
        halves.append(split(z))
    done = {}
    for k in reversed(range(blocks)):
        z = dot3(halves[k], (high[at[k], at[k]], low[at[k], at[k]]))
        for j in range(k + 1, blocks):
            z = z - dot3(done[j], (high[at[k], at[j]], low[at[k], at[j]]), NT)
        z_ref[:, at[k]] = z
        done[k] = split(z)


VMEM = pl.BlockSpec(memory_space=pltpu.VMEM)
LIMIT = 28 << 20


def factor(chunks, n, lo):
    half = jax.ShapeDtypeStruct((n, n), BF16)
    rows = chunks[0].shape[0]
    return pl.pallas_call(
        functools.partial(factor_kernel, lo),
        out_shape=(half, half),
        in_specs=[VMEM] * 8,
        out_specs=(VMEM, VMEM),
        scratch_shapes=[
            pltpu.VMEM((n, n), F32),
            pltpu.VMEM((BLK, BLK), F32),
            pltpu.VMEM((BLK, BLK), F32),
            pltpu.VMEM((n // rows, rows, HALF * rows), F32),
        ],
        compiler_params=pltpu.CompilerParams(vmem_limit_bytes=LIMIT),
        cost_estimate=pl.CostEstimate(flops=COST, bytes_accessed=8 * n * n, transcendentals=0),
        name="factor",
    )(*chunks)


def spread(refs, lo, hi, target, rows):
    own, r, l, top, bottom, xown, xrl, xf = refs
    parts = [own, r, l, (top, bottom), xown, xrl.at[pl.ds(0, rows)], xrl.at[pl.ds(rows, rows)], xf]
    for place, part in zip(places(lax.axis_index("row")), parts):
        ref = target(place)
        if isinstance(part, tuple):
            ref[: rows // 2] = part[0][:, lo:hi]
            ref[rows // 2 :] = part[1][:, lo:hi]
        else:
            ref[...] = part[:, lo:hi]


def earlier_kernel(high, low, *refs):
    chunks, (out, whole_h, whole_l, across, z_ref, l_ref, s_ref) = refs[:8], refs[8:]
    rows, n = out.shape[0], high.shape[0]
    row = lax.axis_index("row")
    z_ref[...] = chunks[0][:, :n]
    spread(chunks, 0, n, lambda place: l_ref.at[span(place, rows)], rows)
    spread(chunks, n, out.shape[1], lambda place: s_ref.at[span(place, rows)], rows)
    for k in range(n // rows):
        ks = slice(k * rows, (k + 1) * rows)
        whole_h[ks, :], whole_l[ks, :] = split(l_ref[ks, :])
        across[:, ks] = l_ref[ks, span(row, rows)].T
    solve(z_ref, high, low)
    g = split(z_ref[...])

    @pl.loop(0, n // BLK)
    def _(j):
        out[:, span(j)] = dot3(g, (whole_h[span(j), :], whole_l[span(j), :]), NT)

    out[:, n:] = dot3(g, split(s_ref[...]))


def later_kernel(high, low, prior, whole_h, whole_l, across, *refs):
    sides, (coupling, term, z_ref, s_ref) = refs[:8], refs[8:]
    rows, n = coupling.shape[0], high.shape[0]
    z_ref[:rows] = prior[...]
    z_ref[rows:] = across[...]
    spread(sides, sides[0].shape[1] - s_ref.shape[1], sides[0].shape[1], lambda place: s_ref.at[span(place, rows)], rows)
    solve(z_ref, high, low)
    h = split(z_ref[...])

    @pl.loop(0, n // BLK)
    def _(j):
        both = dot3(h, (whole_h[:, span(j)], whole_l[:, span(j)]))
        coupling[:, span(j)] = -both[:rows]
        term[:, span(j)] = both[rows:]

    term[:, n:] = dot3((h[0][rows:], h[1][rows:]), split(s_ref[...]))


def pack_kernel(pivot, link, side, half, halfside, linkside):
    rows, n = pivot.shape
    row = lax.axis_index("row")
    for m in range(HALF):
        block = pivot[:, span(lax.rem(row + m, n // rows), rows)]
        half[:, m * rows:(m + 1) * rows] = block
        halfside[:, m * rows:(m + 1) * rows] = block
    halfside[:, HALF * rows:] = side[...]
    linkside[:, :n] = link[...]
    linkside[:, n:] = side[...]


def pack(pivot, link, side):
    rows, n = pivot.shape
    cols = side.shape[1]
    return pl.pallas_call(
        pack_kernel,
        out_shape=tuple(jax.ShapeDtypeStruct((rows, w), F32) for w in (HALF * rows, HALF * rows + cols, n + cols)),
        in_specs=[VMEM] * 3,
        out_specs=(VMEM,) * 3,
        compiler_params=pltpu.CompilerParams(vmem_limit_bytes=8 << 20),
        cost_estimate=pl.CostEstimate(flops=rows * n, bytes_accessed=8 * rows * n, transcendentals=0),
        name="pack",
    )(pivot, link, side)


def earlier(x, chunks, cols):
    n = x[0].shape[0]
    rows = chunks[0].shape[0]
    width = n + cols
    half = jax.ShapeDtypeStruct((n, n), BF16)
    return pl.pallas_call(
        earlier_kernel,
        out_shape=(jax.ShapeDtypeStruct((rows, width), F32), half, half, jax.ShapeDtypeStruct((rows, n), F32)),
        in_specs=[VMEM] * 10,
        out_specs=(VMEM,) * 4,
        scratch_shapes=[pltpu.VMEM((rows, n), F32), pltpu.VMEM((n, n), F32), pltpu.VMEM((n, width - n), F32)],
        compiler_params=pltpu.CompilerParams(vmem_limit_bytes=LIMIT),
        cost_estimate=pl.CostEstimate(flops=COST, bytes_accessed=8 * n * n, transcendentals=0),
        name="earlier",
    )(*x, *chunks)


def later(x, prior, whole, sides, cols):
    n = x[0].shape[0]
    rows = sides[0].shape[0]
    width = n + cols
    return pl.pallas_call(
        later_kernel,
        out_shape=(jax.ShapeDtypeStruct((rows, n), F32), jax.ShapeDtypeStruct((rows, width), F32)),
        in_specs=[VMEM] * 14,
        out_specs=(VMEM, VMEM),
        scratch_shapes=[pltpu.VMEM((2 * rows, n), F32), pltpu.VMEM((n, cols), F32)],
        compiler_params=pltpu.CompilerParams(vmem_limit_bytes=LIMIT),
        cost_estimate=pl.CostEstimate(flops=COST, bytes_accessed=8 * n * n, transcendentals=0),
        name="later",
    )(*x, prior, *whole, *sides)


def together(*values):
    return lax.optimization_barrier(values)


def send(value, to):
    return lax.ppermute(value, "row", [(i, to(i)) for i in range(8)])


def gather_start(rows):
    return rows, send(rows, lambda i: (i + 2) % 8), send(rows, lambda i: (i - 2) % 8), send(rows, lambda i: i ^ 1)


def gather_across(rows, r, l):
    cut = rows.shape[0] // 2
    return send(r[:cut], lambda i: (i + 2) % 8), send(l[cut:], lambda i: (i - 2) % 8)


def gather_swap(rows, r, l, xown, top, bottom):
    xrl = send(jnp.concatenate([r, l]), lambda i: i ^ 1)
    xf = send(jnp.concatenate([top, bottom]), lambda i: i ^ 1)
    return rows, r, l, top, bottom, xown, xrl, xf


def gather_rest(rows, r, l, xown):
    return gather_swap(rows, r, l, xown, *gather_across(rows, r, l))


def local(precisions, couplings, right_sides):
    pivot, link, side = precisions[0], couplings[0], right_sides[0]
    n = pivot.shape[1]
    count = lax.axis_size("tm")
    link = jnp.where(lax.axis_index("tm") == 0, jnp.zeros_like(link), link)
    for level in range(LEVELS):
        h = 1 << level
        ring = [(i, (i + h) % count) for i in range(count)]
        line = [(i, i - h) for i in range(h, count)]
        half, halfside, linkside = pack(pivot, link, side)
        before = lax.ppermute(halfside, "tm", ring)
        first = gather_start(half)
        across = gather_across(*first[:3])
        second = gather_start(together(jnp.concatenate([linkside, before], axis=1), *across)[0])
        before_link = together(link, before)[0]
        x = factor(gather_swap(*first, *across), n, 0)
        *second, before_link, x = together(*second, before_link, x)
        before_l = lax.ppermute(before_link, "tm", ring)
        own = gather_rest(*second)
        sent, *whole = earlier(x, own, side.shape[1])
        got = lax.ppermute(sent, "tm", line)
        *own, sent = together(*own, sent)
        x = factor(own, n, linkside.shape[1])
        link, term = later(x, before_l, whole, own, side.shape[1])
        pivot = pivot - got[:, :n] - term[:, :n]
        side = side - got[:, n:] - term[:, n:]
    return pivot[None], link[None], side[None]


def solution(mesh):
    placed = (P("tm", "row", None),) * 3
    return jax.shard_map(local, mesh=mesh, in_specs=placed, out_specs=placed, check_vma=False)
```

```python
import functools
import jax
import jax.numpy as jnp
from jax import lax
from jax.experimental import pallas as pl
from jax.experimental.pallas import tpu as pltpu
from jax.sharding import PartitionSpec as P

LEVELS = 2
BLK = 256
HALF = 5
COST = 1 << 33
F32, BF16 = jnp.float32, jnp.bfloat16
OFFSETS = ((0, 0), (-1, 0), (1, 0), (2, 0), (0, 1), (-1, 1), (1, 1), (2, 1))
NN, NT, TN = (((1,), (0,)), ((), ())), (((1,), (1,)), ((), ())), (((0,), (0,)), ((), ()))


def split(x):
    high = x.astype(BF16)
    return high, (x - high.astype(F32)).astype(BF16)


def dot(a, b, dims):
    return lax.dot_general(a, b, dims, preferred_element_type=F32)


def dot3(a, b, dims=NN):
    (ah, al), (bh, bl) = a, b
    return dot(ah, bh, dims) + (dot(ah, bl, dims) + dot(al, bh, dims))


def places(row):
    chip, core = row // 2, row % 2
    return [((chip + dx + 4) % 4) * 2 + (core if dc == 0 else 1 - core) for dx, dc in OFFSETS]


def eye(n):
    return (lax.broadcasted_iota(jnp.int32, (n, n), 0) == lax.broadcasted_iota(jnp.int32, (n, n), 1)).astype(F32)


def invert_small(block, x_ref, e_ref):
    one = eye(block.shape[0])
    top = jnp.max(jnp.sum(jnp.abs(block), axis=0))
    scale = 2.0 / (1.0 + top)
    bound = (top - 1.0) / (top + 1.0)
    square = bound * bound
    gain = 2.0 / (2.0 - square)
    e = one - scale * block
    es = split(e)
    x_ref[...] = (gain * scale) * (one + e)
    e_ref[...] = gain * dot3(es, es) + (1.0 - gain) * one

    def coupled(carry):
        count, bound = carry
        square = bound * bound
        gain = 2.0 / (2.0 - square)
        x, e = x_ref[...], e_ref[...]
        es = split(e)
        x_ref[...] = gain * (x + dot3(split(x), es))
        e_ref[...] = gain * dot3(es, es) + (1.0 - gain) * one
        return count + 1, square / (2.0 - square)

    lax.while_loop(lambda c: (c[0] < 40) & (c[1] > 1e-3), coupled, (0, square / (2.0 - square)))

    def residual(carry):
        count, _ = carry
        x = x_ref[...]
        xs = split(x)
        e = one - dot3(xs, split(block))
        x_ref[...] = x + dot3(xs, split(e))
        return count + 1, jnp.max(jnp.sum(jnp.abs(e), axis=0))

    lax.while_loop(lambda c: (c[0] < 20) & (c[1] > 1e-2), residual, (0, jnp.float32(1.0)))


def span(k, size=BLK):
    return pl.ds(pl.multiple_of(k * size, size), size)


def solve(z_ref, high, low):
    blocks = z_ref.shape[1] // BLK
    at = [slice(k * BLK, (k + 1) * BLK) for k in range(blocks)]
    halves = []
    for k in range(blocks):
        z = z_ref[:, at[k]]
        for i in range(k):
            z = z - dot3(halves[i], (high[at[i], at[k]], low[at[i], at[k]]))
        halves.append(split(z))
    done = {}
    for k in reversed(range(blocks)):
        z = dot3(halves[k], (high[at[k], at[k]], low[at[k], at[k]]))
        for j in range(k + 1, blocks):
            z = z - dot3(done[j], (high[at[k], at[j]], low[at[k], at[j]]), NT)
        z_ref[:, at[k]] = z
        done[k] = split(z)


def product_kernel(lo, at, given, *refs):
    chunks, (out, high, low, a_ref, x_ref, e_ref, rows_ref) = refs[:7], refs[7:]
    n, rows, count = a_ref.shape[0], chunks[0].shape[0], rows_ref.shape[0]
    spread(chunks, lo, lo + HALF * rows, lambda place: rows_ref.at[place], rows)
    for k in range(count):
        for m in range(HALF):
            c = (k + m) % count
            block = rows_ref.at[k, :, m * rows:(m + 1) * rows]
            ki, ci = slice(k * rows, (k + 1) * rows), slice(c * rows, (c + 1) * rows)
            if c >= k:
                a_ref[ki, ci] = block[...]
            if (c < k and 2 * m < count) or (c == k + 1 and k % 2 == 0):
                a_ref[ci, ki] = block[...].T
    blocks = n // BLK

    @pl.loop(0, blocks)
    def _(k):
        ks = span(k)
        invert_small(a_ref[ks, ks], x_ref, e_ref)
        xs = split(x_ref[...])
        high[ks, ks], low[ks, ks] = xs

        @pl.loop(k + 1, blocks)
        def _(j):
            js = span(j)
            high[ks, js], low[ks, js] = split(dot3(xs, split(a_ref[ks, js])))

        @pl.loop(k + 1, blocks)
        def _(i):
            side = split(a_ref[ks, span(i)])

            @pl.loop(i, blocks)
            def _(j):
                js = span(j)
                a_ref[span(i), js] = a_ref[span(i), js] - dot3(side, (high[ks, js], low[ks, js]), TN)

    out[...] = given[:, at:at + n]
    solve(out, high, low)


VMEM = pl.BlockSpec(memory_space=pltpu.VMEM)
LIMIT = 28 << 20


def product(given, at, chunks, n, lo, cost):
    rows = chunks[0].shape[0]
    return pl.pallas_call(
        functools.partial(product_kernel, lo, at),
        out_shape=jax.ShapeDtypeStruct((rows, n), F32),
        in_specs=[VMEM] * 8,
        out_specs=VMEM,
        scratch_shapes=[
            pltpu.VMEM((n, n), BF16),
            pltpu.VMEM((n, n), BF16),
            pltpu.VMEM((n, n), F32),
            pltpu.VMEM((BLK, BLK), F32),
            pltpu.VMEM((BLK, BLK), F32),
            pltpu.VMEM((n // rows, rows, HALF * rows), F32),
        ],
        compiler_params=pltpu.CompilerParams(vmem_limit_bytes=LIMIT),
        cost_estimate=pl.CostEstimate(flops=cost, bytes_accessed=8 * n * n, transcendentals=0),
        name="product",
    )(given, *chunks)


def spread(refs, lo, hi, target, rows, skip=0):
    own, r, l, top, bottom, near, xf = refs
    own, r, l = (ref.at[:, skip:] for ref in (own, r, l))
    parts = [own, r, l, (top, bottom), *(near.at[pl.ds(i * rows, rows)] for i in range(3)), xf]
    for place, part in zip(places(lax.axis_index("row")), parts):
        ref = target(place)
        if isinstance(part, tuple):
            ref[: rows // 2] = part[0][:, lo:hi]
            ref[rows // 2 :] = part[1][:, lo:hi]
        else:
            ref[...] = part[:, lo:hi]


def earlier_kernel(given, *refs):
    chunks, (out, whole_h, whole_l, across, l_ref, s_ref) = refs[:7], refs[7:]
    rows, n = given.shape
    row = lax.axis_index("row")
    skip = HALF * rows
    spread(chunks, 0, n, lambda place: l_ref.at[span(place, rows)], rows, skip)
    spread(chunks, n, out.shape[1], lambda place: s_ref.at[span(place, rows)], rows, skip)
    for k in range(n // rows):
        ks = slice(k * rows, (k + 1) * rows)
        whole_h[ks, :], whole_l[ks, :] = split(l_ref[ks, :])
        across[:, ks] = l_ref[ks, span(row, rows)].T
    g = split(given[...])

    @pl.loop(0, n // BLK)
    def _(j):
        out[:, span(j)] = dot3(g, (whole_h[span(j), :], whole_l[span(j), :]), NT)

    out[:, n:] = dot3(g, split(s_ref[...]))


def later_kernel(given, mine, whole_h, whole_l, *refs):
    sides, (coupling, term, s_ref) = refs[:7], refs[7:]
    rows, n = coupling.shape
    spread(sides, HALF * rows, HALF * rows + s_ref.shape[1], lambda place: s_ref.at[span(place, rows)], rows)
    g, h = split(given[...]), split(mine[...])
    both = [jnp.concatenate(pair) for pair in zip(g, h)]

    @pl.loop(0, n // BLK)
    def _(j):
        out = dot3(both, (whole_h[:, span(j)], whole_l[:, span(j)]))
        coupling[:, span(j)] = -out[:rows]
        term[:, span(j)] = out[rows:]

    term[:, n:] = dot3(h, split(s_ref[...]))


def pack_kernel(pivot, link, side, every, halfside):
    rows, n = pivot.shape
    row = lax.axis_index("row")
    for m in range(HALF):
        block = pivot[:, span(lax.rem(row + m, n // rows), rows)]
        every[:, m * rows:(m + 1) * rows] = block
        halfside[:, m * rows:(m + 1) * rows] = block
    halfside[:, HALF * rows:] = side[...]
    every[:, HALF * rows:HALF * rows + n] = link[...]
    every[:, HALF * rows + n:] = side[...]


def pack(pivot, link, side):
    rows, n = pivot.shape
    cols = side.shape[1]
    return pl.pallas_call(
        pack_kernel,
        out_shape=tuple(jax.ShapeDtypeStruct((rows, w), F32) for w in (HALF * rows + n + cols, HALF * rows + cols)),
        in_specs=[VMEM] * 3,
        out_specs=(VMEM,) * 2,
        compiler_params=pltpu.CompilerParams(vmem_limit_bytes=8 << 20),
        cost_estimate=pl.CostEstimate(flops=rows * n, bytes_accessed=8 * rows * n, transcendentals=0),
        name="pack",
    )(pivot, link, side)


def earlier(given, chunks, cols):
    rows, n = given.shape
    half = jax.ShapeDtypeStruct((n, n), BF16)
    return pl.pallas_call(
        earlier_kernel,
        out_shape=(jax.ShapeDtypeStruct((rows, n + cols), F32), half, half, jax.ShapeDtypeStruct((rows, n), F32)),
        in_specs=[VMEM] * 8,
        out_specs=(VMEM,) * 4,
        scratch_shapes=[pltpu.VMEM((n, n), F32), pltpu.VMEM((n, cols), F32)],
        compiler_params=pltpu.CompilerParams(vmem_limit_bytes=LIMIT),
        cost_estimate=pl.CostEstimate(flops=COST, bytes_accessed=8 * n * n, transcendentals=0),
        name="earlier",
    )(given, *chunks)


def later(given, mine, whole, sides, cols):
    rows, n = given.shape
    return pl.pallas_call(
        later_kernel,
        out_shape=(jax.ShapeDtypeStruct((rows, n), F32), jax.ShapeDtypeStruct((rows, n + cols), F32)),
        in_specs=[VMEM] * 11,
        out_specs=(VMEM, VMEM),
        scratch_shapes=[pltpu.VMEM((n, cols), F32)],
        compiler_params=pltpu.CompilerParams(vmem_limit_bytes=LIMIT),
        cost_estimate=pl.CostEstimate(flops=COST >> 12, bytes_accessed=8 * n * n, transcendentals=0),
        name="later",
    )(given, mine, *whole, *sides)


def together(*values):
    return lax.optimization_barrier(values)


def send(value, to):
    return lax.ppermute(value, "row", [(i, to(i)) for i in range(8)])


def gather_near(rows):
    return rows, send(rows, lambda i: (i + 2) % 8), send(rows, lambda i: (i - 2) % 8)


def gather_far(rows, r, l):
    cut = rows.shape[0] // 2
    return send(r[:cut], lambda i: (i + 2) % 8), send(l[cut:], lambda i: (i - 2) % 8)


def swap(*values):
    return send(jnp.concatenate(values), lambda i: i ^ 1)


def local(precisions, couplings, right_sides):
    pivot, link, side = precisions[0], couplings[0], right_sides[0]
    n = pivot.shape[1]
    count = lax.axis_size("tm")
    link = jnp.where(lax.axis_index("tm") == 0, jnp.zeros_like(link), link)
    for level in range(LEVELS):
        h = 1 << level
        ring = [(i, (i + h) % count) for i in range(count)]
        line = [(i, i - h) for i in range(h, count)]
        every, halfside = pack(pivot, link, side)
        cut = halfside.shape[1] - side.shape[1]
        before = lax.ppermute(halfside, "tm", ring)
        first = gather_near(every)
        *first, before = together(*first, before)
        head, tail = [v[:, :cut] for v in first], [v[:, cut:] for v in first]
        far = gather_far(*head)
        own = (*first, *gather_far(*tail), swap(*tail))
        third = gather_near(before)
        mine = product(every, cut, (*first, *far, swap(*head), swap(*far)), n, 0, COST)
        *rest, mine = together(*own, *third, mine)
        own, third = rest[:6], rest[6:]
        theirs = lax.ppermute(mine, "tm", ring)
        far = gather_far(*third)
        near = swap(*third)
        sent, *whole, across = earlier(mine, (*own, swap(*own[3:5])), side.shape[1])
        got = lax.ppermute(sent, "tm", line)
        *prior, _ = together(*third, *far, near, sent)
        prior = (*prior, swap(*prior[3:5]))
        mine = product(across, 0, prior, n, 0, COST >> 12)
        link, term = later(theirs, mine, whole, prior, side.shape[1])
        pivot = pivot - got[:, :n] - term[:, :n]
        side = side - got[:, n:] - term[:, n:]
    return pivot[None], link[None], side[None]


def solution(mesh):
    placed = (P("tm", "row", None),) * 3
    return jax.shard_map(local, mesh=mesh, in_specs=placed, out_specs=placed, check_vma=False)
```

```python
import functools
import jax
import jax.numpy as jnp
from jax import lax
from jax.experimental import pallas as pl
from jax.experimental.pallas import tpu as pltpu
from jax.sharding import PartitionSpec as P

LEVELS = 2
BLK = 256
HALF = 5
COST = 1 << 33
F32, BF16 = jnp.float32, jnp.bfloat16
OFFSETS = ((0, 0), (-1, 0), (1, 0), (2, 0), (0, 1), (-1, 1), (1, 1), (2, 1))
NN, NT, TN = (((1,), (0,)), ((), ())), (((1,), (1,)), ((), ())), (((0,), (0,)), ((), ()))


def split(x):
    high = x.astype(BF16)
    return high, (x - high.astype(F32)).astype(BF16)


def dot(a, b, dims):
    return lax.dot_general(a, b, dims, preferred_element_type=F32)


def dot3(a, b, dims=NN):
    (ah, al), (bh, bl) = a, b
    return dot(ah, bh, dims) + (dot(ah, bl, dims) + dot(al, bh, dims))


def places(row):
    chip, core = row // 2, row % 2
    return [((chip + dx + 4) % 4) * 2 + (core if dc == 0 else 1 - core) for dx, dc in OFFSETS]


def eye(n):
    return (lax.broadcasted_iota(jnp.int32, (n, n), 0) == lax.broadcasted_iota(jnp.int32, (n, n), 1)).astype(F32)


def invert_small(block, x_ref, e_ref):
    one = eye(block.shape[0])
    top = jnp.max(jnp.sum(jnp.abs(block), axis=0))
    scale = 2.0 / (1.0 + top)
    bound = (top - 1.0) / (top + 1.0)
    square = bound * bound
    gain = 2.0 / (2.0 - square)
    e = one - scale * block
    es = split(e)
    x_ref[...] = (gain * scale) * (one + e)
    e_ref[...] = gain * dot3(es, es) + (1.0 - gain) * one

    def coupled(carry):
        count, bound = carry
        square = bound * bound
        gain = 2.0 / (2.0 - square)
        x, e = x_ref[...], e_ref[...]
        es = split(e)
        x_ref[...] = gain * (x + dot3(split(x), es))
        e_ref[...] = gain * dot3(es, es) + (1.0 - gain) * one
        return count + 1, square / (2.0 - square)

    lax.while_loop(lambda c: (c[0] < 40) & (c[1] > 1e-3), coupled, (0, square / (2.0 - square)))

    def residual(carry):
        count, _ = carry
        x = x_ref[...]
        xs = split(x)
        e = one - dot3(xs, split(block))
        x_ref[...] = x + dot3(xs, split(e))
        return count + 1, jnp.max(jnp.sum(jnp.abs(e), axis=0))

    lax.while_loop(lambda c: (c[0] < 20) & (c[1] > 1e-2), residual, (0, jnp.float32(1.0)))


def span(k, size=BLK):
    return pl.ds(pl.multiple_of(k * size, size), size)


def solve(z_ref, high, low):
    blocks = z_ref.shape[1] // BLK
    at = [slice(k * BLK, (k + 1) * BLK) for k in range(blocks)]
    halves = []
    for k in range(blocks):
        z = z_ref[:, at[k]]
        for i in range(k):
            z = z - dot3(halves[i], (high[at[i], at[k]], low[at[i], at[k]]))
        halves.append(split(z))
    done = {}
    for k in reversed(range(blocks)):
        z = dot3(halves[k], (high[at[k], at[k]], low[at[k], at[k]]))
        for j in range(k + 1, blocks):
            z = z - dot3(done[j], (high[at[k], at[j]], low[at[k], at[j]]), NT)
        z_ref[:, at[k]] = z
        done[k] = split(z)


def product_kernel(lo, at, given, *refs):
    chunks, (out, high, low, a_ref, x_ref, e_ref, rows_ref) = refs[:7], refs[7:]
    n, rows, count = a_ref.shape[0], chunks[0].shape[0], rows_ref.shape[0]
    spread(chunks, lo, lo + HALF * rows, lambda place: rows_ref.at[place], rows)
    for k in range(count):
        for m in range(HALF):
            c = (k + m) % count
            block = rows_ref.at[k, :, m * rows:(m + 1) * rows]
            ki, ci = slice(k * rows, (k + 1) * rows), slice(c * rows, (c + 1) * rows)
            if c >= k:
                a_ref[ki, ci] = block[...]
            if (c < k and 2 * m < count) or (c == k + 1 and k % 2 == 0):
                a_ref[ci, ki] = block[...].T
    blocks = n // BLK

    @pl.loop(0, blocks)
    def _(k):
        ks = span(k)
        invert_small(a_ref[ks, ks], x_ref, e_ref)
        xs = split(x_ref[...])
        high[ks, ks], low[ks, ks] = xs

        @pl.loop(k + 1, blocks)
        def _(j):
            js = span(j)
            high[ks, js], low[ks, js] = split(dot3(xs, split(a_ref[ks, js])))

        @pl.loop(k + 1, blocks)
        def _(i):
            side = split(a_ref[ks, span(i)])

            @pl.loop(i, blocks)
            def _(j):
                js = span(j)
                a_ref[span(i), js] = a_ref[span(i), js] - dot3(side, (high[ks, js], low[ks, js]), TN)

    out[...] = given[:, at:at + n]
    solve(out, high, low)


VMEM = pl.BlockSpec(memory_space=pltpu.VMEM)
LIMIT = 28 << 20


def product(given, at, chunks, n, lo, cost):
    rows = chunks[0].shape[0]
    return pl.pallas_call(
        functools.partial(product_kernel, lo, at),
        out_shape=jax.ShapeDtypeStruct((rows, n), F32),
        in_specs=[VMEM] * 8,
        out_specs=VMEM,
        scratch_shapes=[
            pltpu.VMEM((n, n), BF16),
            pltpu.VMEM((n, n), BF16),
            pltpu.VMEM((n, n), F32),
            pltpu.VMEM((BLK, BLK), F32),
            pltpu.VMEM((BLK, BLK), F32),
            pltpu.VMEM((n // rows, rows, HALF * rows), F32),
        ],
        compiler_params=pltpu.CompilerParams(vmem_limit_bytes=LIMIT),
        cost_estimate=pl.CostEstimate(flops=cost, bytes_accessed=8 * n * n, transcendentals=0),
        name="product",
    )(given, *chunks)


def spread(refs, lo, hi, target, rows, skip=0):
    own, r, l, top, bottom, near, xf = refs
    own, r, l = (ref.at[:, skip:] for ref in (own, r, l))
    parts = [own, r, l, (top, bottom), *(near.at[pl.ds(i * rows, rows)] for i in range(3)), xf]
    for place, part in zip(places(lax.axis_index("row")), parts):
        ref = target(place)
        if isinstance(part, tuple):
            ref[: rows // 2] = part[0][:, lo:hi]
            ref[rows // 2 :] = part[1][:, lo:hi]
        else:
            ref[...] = part[:, lo:hi]


def earlier_kernel(given, *refs):
    chunks, (out, whole_h, whole_l, across, l_ref, s_ref) = refs[:7], refs[7:]
    rows, n = given.shape
    row = lax.axis_index("row")
    skip = HALF * rows
    spread(chunks, 0, n, lambda place: l_ref.at[span(place, rows)], rows, skip)
    spread(chunks, n, out.shape[1], lambda place: s_ref.at[span(place, rows)], rows, skip)

    @pl.loop(0, n // rows)
    def _(k):
        ks = span(k, rows)
        whole_h[ks, :], whole_l[ks, :] = split(l_ref[ks, :])
        across[:, ks] = l_ref[ks, span(row, rows)].T

    g = split(given[...])

    @pl.loop(0, n // BLK)
    def _(j):
        out[:, span(j)] = dot3(g, (whole_h[span(j), :], whole_l[span(j), :]), NT)

    out[:, n:] = dot3(g, split(s_ref[...]))


def later_kernel(given, mine, whole_h, whole_l, *refs):
    sides, (coupling, term, s_ref) = refs[:7], refs[7:]
    rows, n = coupling.shape
    spread(sides, HALF * rows, HALF * rows + s_ref.shape[1], lambda place: s_ref.at[span(place, rows)], rows)
    g, h = split(given[...]), split(mine[...])
    both = [jnp.concatenate(pair) for pair in zip(g, h)]

    @pl.loop(0, n // BLK)
    def _(j):
        out = dot3(both, (whole_h[:, span(j)], whole_l[:, span(j)]))
        coupling[:, span(j)] = -out[:rows]
        term[:, span(j)] = out[rows:]

    term[:, n:] = dot3(h, split(s_ref[...]))


def pack_kernel(pivot, link, side, every, halfside):
    rows, n = pivot.shape
    row = lax.axis_index("row")
    for m in range(HALF):
        block = pivot[:, span(lax.rem(row + m, n // rows), rows)]
        every[:, m * rows:(m + 1) * rows] = block
        halfside[:, m * rows:(m + 1) * rows] = block
    halfside[:, HALF * rows:] = side[...]
    every[:, HALF * rows:HALF * rows + n] = link[...]
    every[:, HALF * rows + n:] = side[...]


def pack(pivot, link, side):
    rows, n = pivot.shape
    cols = side.shape[1]
    return pl.pallas_call(
        pack_kernel,
        out_shape=tuple(jax.ShapeDtypeStruct((rows, w), F32) for w in (HALF * rows + n + cols, HALF * rows + cols)),
        in_specs=[VMEM] * 3,
        out_specs=(VMEM,) * 2,
        compiler_params=pltpu.CompilerParams(vmem_limit_bytes=8 << 20),
        cost_estimate=pl.CostEstimate(flops=rows * n, bytes_accessed=8 * rows * n, transcendentals=0),
        name="pack",
    )(pivot, link, side)


def earlier(given, chunks, cols):
    rows, n = given.shape
    half = jax.ShapeDtypeStruct((n, n), BF16)
    return pl.pallas_call(
        earlier_kernel,
        out_shape=(jax.ShapeDtypeStruct((rows, n + cols), F32), half, half, jax.ShapeDtypeStruct((rows, n), F32)),
        in_specs=[VMEM] * 8,
        out_specs=(VMEM,) * 4,
        scratch_shapes=[pltpu.VMEM((n, n), F32), pltpu.VMEM((n, cols), F32)],
        compiler_params=pltpu.CompilerParams(vmem_limit_bytes=LIMIT),
        cost_estimate=pl.CostEstimate(flops=COST, bytes_accessed=8 * n * n, transcendentals=0),
        name="earlier",
    )(given, *chunks)


def later(given, mine, whole, sides, cols):
    rows, n = given.shape
    return pl.pallas_call(
        later_kernel,
        out_shape=(jax.ShapeDtypeStruct((rows, n), F32), jax.ShapeDtypeStruct((rows, n + cols), F32)),
        in_specs=[VMEM] * 11,
        out_specs=(VMEM, VMEM),
        scratch_shapes=[pltpu.VMEM((n, cols), F32)],
        compiler_params=pltpu.CompilerParams(vmem_limit_bytes=LIMIT),
        cost_estimate=pl.CostEstimate(flops=COST >> 12, bytes_accessed=8 * n * n, transcendentals=0),
        name="later",
    )(given, mine, *whole, *sides)


def carry_kernel(given, out):
    out[...] = given[...]


def carry(given):
    return pl.pallas_call(
        carry_kernel,
        out_shape=jax.ShapeDtypeStruct(given.shape, F32),
        in_specs=[VMEM],
        out_specs=VMEM,
        compiler_params=pltpu.CompilerParams(vmem_limit_bytes=4 << 20),
        cost_estimate=pl.CostEstimate(flops=COST, bytes_accessed=8 * given.size, transcendentals=0),
        name="carry",
    )(given)


def together(*values):
    return lax.optimization_barrier(values)


def send(value, to):
    return lax.ppermute(value, "row", [(i, to(i)) for i in range(8)])


def gather_near(rows):
    return rows, send(rows, lambda i: (i + 2) % 8), send(rows, lambda i: (i - 2) % 8)


def gather_far(rows, r, l):
    cut = rows.shape[0] // 2
    return send(r[:cut], lambda i: (i + 2) % 8), send(l[cut:], lambda i: (i - 2) % 8)


def swap(*values):
    return send(jnp.concatenate(values), lambda i: i ^ 1)


def local(precisions, couplings, right_sides):
    pivot, link, side = precisions[0], couplings[0], right_sides[0]
    n = pivot.shape[1]
    count = lax.axis_size("tm")
    link = jnp.where(lax.axis_index("tm") == 0, jnp.zeros_like(link), link)
    for level in range(LEVELS):
        h = 1 << level
        ring = [(i, (i + h) % count) for i in range(count)]
        line = [(i, i - h) for i in range(h, count)]
        every, halfside = pack(pivot, link, side)
        cut = halfside.shape[1] - side.shape[1]
        before = lax.ppermute(halfside, "tm", ring)
        first = gather_near(every)
        *first, before = together(*first, carry(before) if h > 1 else before)
        head, tail = [v[:, :cut] for v in first], [v[:, cut:] for v in first]
        far = gather_far(*head)
        own = (*first, *gather_far(*tail), swap(*tail))
        third = gather_near(before)
        mine = product(every, cut, (*first, *far, swap(*head), swap(*far)), n, 0, COST)
        *rest, mine = together(*own, *third, mine)
        own, third = rest[:6], rest[6:]
        theirs = lax.ppermute(mine, "tm", ring)
        far = gather_far(*third)
        near = swap(*third)
        sent, *whole, across = earlier(mine, (*own, swap(*own[3:5])), side.shape[1])
        got = lax.ppermute(sent, "tm", line)
        *prior, _ = together(*third, *far, near, sent)
        prior = (*prior, swap(*prior[3:5]))
        mine = product(across, 0, prior, n, 0, COST >> 12)
        link, term = later(theirs, mine, whole, prior, side.shape[1])
        pivot = pivot - got[:, :n] - term[:, :n]
        side = side - got[:, n:] - term[:, n:]
    return pivot[None], link[None], side[None]


def solution(mesh):
    placed = (P("tm", "row", None),) * 3
    return jax.shard_map(local, mesh=mesh, in_specs=placed, out_specs=placed, check_vma=False)
```

```python
import functools
import jax
import jax.numpy as jnp
from jax import lax
from jax.experimental import pallas as pl
from jax.experimental.pallas import tpu as pltpu
from jax.sharding import PartitionSpec as P

LEVELS = 2
BLK = 256
HALF = 5
COST = 1 << 33
F32, BF16 = jnp.float32, jnp.bfloat16
OFFSETS = ((0, 0), (-1, 0), (1, 0), (2, 0), (0, 1), (-1, 1), (1, 1), (2, 1))
NN, NT, TN = (((1,), (0,)), ((), ())), (((1,), (1,)), ((), ())), (((0,), (0,)), ((), ()))


def split(x):
    high = x.astype(BF16)
    return high, (x - high.astype(F32)).astype(BF16)


def dot(a, b, dims):
    return lax.dot_general(a, b, dims, preferred_element_type=F32)


def dot3(a, b, dims=NN):
    (ah, al), (bh, bl) = a, b
    return dot(ah, bh, dims) + (dot(ah, bl, dims) + dot(al, bh, dims))


def places(row):
    chip, core = row // 2, row % 2
    return [((chip + dx + 4) % 4) * 2 + (core if dc == 0 else 1 - core) for dx, dc in OFFSETS]


def eye(n):
    return (lax.broadcasted_iota(jnp.int32, (n, n), 0) == lax.broadcasted_iota(jnp.int32, (n, n), 1)).astype(F32)


def invert_small(block, x_ref, e_ref):
    one = eye(block.shape[0])
    top = jnp.max(jnp.sum(jnp.abs(block), axis=0))
    scale = 2.0 / (1.0 + top)
    bound = (top - 1.0) / (top + 1.0)
    square = bound * bound
    gain = 2.0 / (2.0 - square)
    e = one - scale * block
    es = split(e)
    x_ref[...] = (gain * scale) * (one + e)
    e_ref[...] = gain * dot3(es, es) + (1.0 - gain) * one

    def coupled(carry):
        count, bound = carry
        square = bound * bound
        gain = 2.0 / (2.0 - square)
        x, e = x_ref[...], e_ref[...]
        es = split(e)
        x_ref[...] = gain * (x + dot3(split(x), es))
        e_ref[...] = gain * dot3(es, es) + (1.0 - gain) * one
        return count + 1, square / (2.0 - square)

    lax.while_loop(lambda c: (c[0] < 40) & (c[1] > 1e-3), coupled, (0, square / (2.0 - square)))

    def residual(carry):
        count, _ = carry
        x = x_ref[...]
        xs = split(x)
        e = one - dot3(xs, split(block))
        x_ref[...] = x + dot3(xs, split(e))
        return count + 1, jnp.max(jnp.sum(jnp.abs(e), axis=0))

    lax.while_loop(lambda c: (c[0] < 20) & (c[1] > 1e-2), residual, (0, jnp.float32(1.0)))


def span(k, size=BLK):
    return pl.ds(pl.multiple_of(k * size, size), size)


def solve(z_ref, high, low):
    blocks = z_ref.shape[1] // BLK
    at = [slice(k * BLK, (k + 1) * BLK) for k in range(blocks)]
    halves = []
    for k in range(blocks):
        z = z_ref[:, at[k]]
        for i in range(k):
            z = z - dot3(halves[i], (high[at[i], at[k]], low[at[i], at[k]]))
        halves.append(split(z))
    done = {}
    for k in reversed(range(blocks)):
        z = dot3(halves[k], (high[at[k], at[k]], low[at[k], at[k]]))
        for j in range(k + 1, blocks):
            z = z - dot3(done[j], (high[at[k], at[j]], low[at[k], at[j]]), NT)
        z_ref[:, at[k]] = z
        done[k] = split(z)


def product_kernel(lo, at, given, *refs):
    chunks, (out, high, low, a_ref, x_ref, e_ref, rows_ref) = refs[:7], refs[7:]
    n, rows, count = a_ref.shape[0], chunks[0].shape[0], rows_ref.shape[0]
    spread(chunks, lo, lo + HALF * rows, lambda place: rows_ref.at[place], rows)
    for k in range(count):
        for m in range(HALF):
            c = (k + m) % count
            block = rows_ref.at[k, :, m * rows:(m + 1) * rows]
            ki, ci = slice(k * rows, (k + 1) * rows), slice(c * rows, (c + 1) * rows)
            if c >= k:
                a_ref[ki, ci] = block[...]
            if (c < k and 2 * m < count) or (c == k + 1 and k % 2 == 0):
                a_ref[ci, ki] = block[...].T
    blocks = n // BLK

    @pl.loop(0, blocks)
    def _(k):
        ks = span(k)
        invert_small(a_ref[ks, ks], x_ref, e_ref)
        xs = split(x_ref[...])
        high[ks, ks], low[ks, ks] = xs

        @pl.loop(k + 1, blocks)
        def _(j):
            js = span(j)
            high[ks, js], low[ks, js] = split(dot3(xs, split(a_ref[ks, js])))

        @pl.loop(k + 1, blocks)
        def _(i):
            side = split(a_ref[ks, span(i)])

            @pl.loop(i, blocks)
            def _(j):
                js = span(j)
                a_ref[span(i), js] = a_ref[span(i), js] - dot3(side, (high[ks, js], low[ks, js]), TN)

    out[...] = given[:, at:at + n]
    solve(out, high, low)


VMEM = pl.BlockSpec(memory_space=pltpu.VMEM)
LIMIT = 28 << 20


def product(given, at, chunks, n, lo, cost):
    rows = chunks[0].shape[0]
    return pl.pallas_call(
        functools.partial(product_kernel, lo, at),
        out_shape=jax.ShapeDtypeStruct((rows, n), F32),
        in_specs=[VMEM] * 8,
        out_specs=VMEM,
        scratch_shapes=[
            pltpu.VMEM((n, n), BF16),
            pltpu.VMEM((n, n), BF16),
            pltpu.VMEM((n, n), F32),
            pltpu.VMEM((BLK, BLK), F32),
            pltpu.VMEM((BLK, BLK), F32),
            pltpu.VMEM((n // rows, rows, HALF * rows), F32),
        ],
        compiler_params=pltpu.CompilerParams(vmem_limit_bytes=LIMIT),
        cost_estimate=pl.CostEstimate(flops=cost, bytes_accessed=8 * n * n, transcendentals=0),
        name="product",
    )(given, *chunks)


def spread(refs, lo, hi, target, rows, skip=0):
    own, r, l, top, bottom, near, xf = refs
    own, r, l = (ref.at[:, skip:] for ref in (own, r, l))
    parts = [own, r, l, (top, bottom), *(near.at[pl.ds(i * rows, rows)] for i in range(3)), xf]
    for place, part in zip(places(lax.axis_index("row")), parts):
        ref = target(place)
        if isinstance(part, tuple):
            ref[: rows // 2] = part[0][:, lo:hi]
            ref[rows // 2 :] = part[1][:, lo:hi]
        else:
            ref[...] = part[:, lo:hi]


def earlier_kernel(given, *refs):
    chunks, (out, whole_h, whole_l, across, l_ref, s_ref) = refs[:7], refs[7:]
    rows, n = given.shape
    row = lax.axis_index("row")
    skip = HALF * rows
    spread(chunks, 0, n, lambda place: l_ref.at[span(place, rows)], rows, skip)
    spread(chunks, n, out.shape[1], lambda place: s_ref.at[span(place, rows)], rows, skip)

    @pl.loop(0, n // rows)
    def _(k):
        ks = span(k, rows)
        whole_h[ks, :], whole_l[ks, :] = split(l_ref[ks, :])
        across[:, ks] = l_ref[ks, span(row, rows)].T

    g = split(given[...])

    @pl.loop(0, n // BLK)
    def _(j):
        out[:, span(j)] = dot3(g, (whole_h[span(j), :], whole_l[span(j), :]), NT)

    out[:, n:] = dot3(g, split(s_ref[...]))


def later_kernel(given, mine, whole_h, whole_l, *refs):
    sides, (coupling, term, s_ref) = refs[:7], refs[7:]
    rows, n = coupling.shape
    spread(sides, HALF * rows, HALF * rows + s_ref.shape[1], lambda place: s_ref.at[span(place, rows)], rows)
    g, h = split(given[...]), split(mine[...])
    both = [jnp.concatenate(pair) for pair in zip(g, h)]

    @pl.loop(0, n // BLK)
    def _(j):
        out = dot3(both, (whole_h[:, span(j)], whole_l[:, span(j)]))
        coupling[:, span(j)] = -out[:rows]
        term[:, span(j)] = out[rows:]

    term[:, n:] = dot3(h, split(s_ref[...]))


def pack_kernel(pivot, link, side, every, halfside):
    rows, n = pivot.shape
    row = lax.axis_index("row")
    for m in range(HALF):
        block = pivot[:, span(lax.rem(row + m, n // rows), rows)]
        every[:, m * rows:(m + 1) * rows] = block
        halfside[:, m * rows:(m + 1) * rows] = block
    halfside[:, HALF * rows:] = side[...]
    every[:, HALF * rows:HALF * rows + n] = link[...]
    every[:, HALF * rows + n:] = side[...]


def pack(pivot, link, side):
    rows, n = pivot.shape
    cols = side.shape[1]
    return pl.pallas_call(
        pack_kernel,
        out_shape=tuple(jax.ShapeDtypeStruct((rows, w), F32) for w in (HALF * rows + n + cols, HALF * rows + cols)),
        in_specs=[VMEM] * 3,
        out_specs=(VMEM,) * 2,
        compiler_params=pltpu.CompilerParams(vmem_limit_bytes=8 << 20),
        cost_estimate=pl.CostEstimate(flops=rows * n, bytes_accessed=8 * rows * n, transcendentals=0),
        name="pack",
    )(pivot, link, side)


def earlier(given, chunks, cols):
    rows, n = given.shape
    half = jax.ShapeDtypeStruct((n, n), BF16)
    return pl.pallas_call(
        earlier_kernel,
        out_shape=(jax.ShapeDtypeStruct((rows, n + cols), F32), half, half, jax.ShapeDtypeStruct((rows, n), F32)),
        in_specs=[VMEM] * 8,
        out_specs=(VMEM,) * 4,
        scratch_shapes=[pltpu.VMEM((n, n), F32), pltpu.VMEM((n, cols), F32)],
        compiler_params=pltpu.CompilerParams(vmem_limit_bytes=LIMIT),
        cost_estimate=pl.CostEstimate(flops=COST, bytes_accessed=8 * n * n, transcendentals=0),
        name="earlier",
    )(given, *chunks)


def later(given, mine, whole, sides, cols):
    rows, n = given.shape
    return pl.pallas_call(
        later_kernel,
        out_shape=(jax.ShapeDtypeStruct((rows, n), F32), jax.ShapeDtypeStruct((rows, n + cols), F32)),
        in_specs=[VMEM] * 11,
        out_specs=(VMEM, VMEM),
        scratch_shapes=[pltpu.VMEM((n, cols), F32)],
        compiler_params=pltpu.CompilerParams(vmem_limit_bytes=LIMIT),
        cost_estimate=pl.CostEstimate(flops=COST >> 12, bytes_accessed=8 * n * n, transcendentals=0),
        name="later",
    )(given, mine, *whole, *sides)


def together(*values):
    return lax.optimization_barrier(values)


def send(value, to):
    return lax.ppermute(value, "row", [(i, to(i)) for i in range(8)])


def gather_near(rows):
    return rows, send(rows, lambda i: (i + 2) % 8), send(rows, lambda i: (i - 2) % 8)


def gather_far(rows, r, l):
    cut = rows.shape[0] // 2
    return send(r[:cut], lambda i: (i + 2) % 8), send(l[cut:], lambda i: (i - 2) % 8)


def swap(*values):
    return send(jnp.concatenate(values), lambda i: i ^ 1)


def local(precisions, couplings, right_sides):
    pivot, link, side = precisions[0], couplings[0], right_sides[0]
    n = pivot.shape[1]
    count = lax.axis_size("tm")
    link = jnp.where(lax.axis_index("tm") == 0, jnp.zeros_like(link), link)
    for level in range(LEVELS):
        h = 1 << level
        ring = [(i, (i + h) % count) for i in range(count)]
        line = [(i, i - h) for i in range(h, count)]
        every, halfside = pack(pivot, link, side)
        cut = halfside.shape[1] - side.shape[1]
        before = lax.ppermute(halfside, "tm", ring)
        first = gather_near(every)
        *first, before = together(*first, before)
        head, tail = [v[:, :cut] for v in first], [v[:, cut:] for v in first]
        far = gather_far(*head)
        own = (*first, *gather_far(*tail), swap(*tail))
        third = gather_near(before)
        mine = product(every, cut, (*first, *far, swap(*head), swap(*far)), n, 0, COST)
        *rest, mine = together(*own, *third, mine)
        own, third = rest[:6], rest[6:]
        theirs = lax.ppermute(mine, "tm", ring)
        far = gather_far(*third)
        near = swap(*third)
        sent, *whole, across = earlier(mine, (*own, swap(*own[3:5])), side.shape[1])
        got = lax.ppermute(sent, "tm", line)
        *prior, _ = together(*third, *far, near, sent)
        prior = (*prior, swap(*prior[3:5]))
        mine = product(across, 0, prior, n, 0, COST >> 12)
        link, term = later(theirs, mine, whole, prior, side.shape[1])
        pivot = pivot - got[:, :n] - term[:, :n]
        side = side - got[:, n:] - term[:, n:]
    return pivot[None], link[None], side[None]


def solution(mesh):
    placed = (P("tm", "row", None),) * 3
    return jax.shard_map(local, mesh=mesh, in_specs=placed, out_specs=placed, check_vma=False)
```
